32 devices in a mesh: gx: 4 (over z), gy: 2 (over x), gz: 4 (over y, core).
Axes of the slice: x: 2, y: 2, z: 4, core: 2. Of those that a mesh axis runs over, the one named last changes fastest.
Arguments:
- volume: bfloat16 [64, 256, 512], P('gz', 'gy', 'gx'), may hold values from 0 to 1
- hat_center: int32 [256], replicated, may hold values from 0 to 255
- tf_table: bfloat16 [4, 256], replicated, may hold values from 0.049804688 to 1
Outputs:
- image: float32 [4, 256, 512], P(None, 'gy')
The draws below stay inside these ranges and needn't reach their ends.
All inputs are finite; a program needn't handle non-finite values.
Results may differ from the reference program's by a relative error of at most 0.0003.
Values may be sent and summed in bfloat16 or wider, within the bound.
A program may use at most 64 MiB of HBM per device.

```python
import math
import jax
import jax.numpy as jnp
from jax import lax

NBIN = 256
HW = 4
NX = 512
NY = 256
NZ = 64


def set_ends(values, stream_key, low, top_value):
    longest = values.shape.index(max(values.shape))
    spots = []
    for shift in (0, 1):
        where = [jax.random.randint(jax.random.fold_in(stream_key, axis), (), 0, length) for axis, length in enumerate(values.shape)]
        where[longest] = (where[longest] + shift) % values.shape[longest]
        spots.append(tuple(where))
    return values.at[spots[0]].set(low).at[spots[1]].set(top_value)


def block_levels(own_key, dims, split, smallest, top_value):
    def one(dim, blocks):
        steps = jax.random.uniform(jax.random.fold_in(jax.random.fold_in(own_key, 6), dim), (blocks,), jnp.float32, smallest / len(split), top_value / len(split))
        return jnp.repeat(jnp.exp(steps), dims[dim] // blocks).reshape((-1,) + (1,) * (len(dims) - dim - 1))

    factor_of = one(*split[0])
    for cut in split[1:]:
        factor_of = factor_of * one(*cut)
    return factor_of


def setup_inputs(seed: int = 0) -> dict:
    splits = jax.random.split(jax.random.key(seed), 4)
    volume = jnp.clip(1.0 * jax.random.uniform(splits[0], (NZ, NY, NX), jnp.float32) ** block_levels(splits[0], (NZ, NY, NX), ((0, 4), (1, 2), (2, 4)), -0.2, 0.2), 0.0, 1.0).astype(jnp.bfloat16)
    hat_center = set_ends(jax.random.randint(splits[1], (NBIN,), 0, NBIN), jax.random.fold_in(splits[1], 1), 0, NBIN - 1).astype(jnp.int32)
    tf_table = jnp.clip(jnp.exp(jax.random.uniform(splits[2], (4, NBIN), jnp.float32, math.log(0.049804688), math.log(1.0))), 0.049804688, 1.0).astype(jnp.bfloat16)
    return dict(volume=volume, hat_center=hat_center, tf_table=tf_table)


ambient = 0.3
grad_floor = 0.01
depth_scale = 1.5

def smooth(values, along):
    length = values.shape[along] - 2
    return lax.slice_in_dim(values, 0, length, axis=along) + 2.0 * lax.slice_in_dim(values, 1, length + 1, axis=along) + lax.slice_in_dim(values, 2, length + 2, axis=along)

def differ(values, along):
    length = values.shape[along] - 2
    return lax.slice_in_dim(values, 2, length + 2, axis=along) - lax.slice_in_dim(values, 0, length, axis=along)

def shading(padded):
    grad_x = smooth(smooth(differ(padded, 2), 1), 0) / 32.0
    grad_y = smooth(smooth(differ(padded, 1), 2), 0) / 32.0
    grad_z = smooth(smooth(differ(padded, 0), 2), 1) / 32.0
    facing = jnp.abs(grad_x + grad_y + grad_z) / jnp.sqrt(3.0)
    length = jnp.sqrt(grad_x * grad_x + grad_y * grad_y + grad_z * grad_z + grad_floor)
    return ambient + (1.0 - ambient) * facing / length

def colour(voxels, centers, tf_table):
    bin_level = voxels.astype(jnp.float32) * (NBIN - 1)
    hat_values = jnp.maximum(0.0, 1.0 - jnp.abs(bin_level[None, :] - centers[:, None]) / HW).astype(jnp.bfloat16)
    return jnp.dot(tf_table, hat_values, preferred_element_type=jnp.float32)

def reference(volume, hat_center, tf_table):
    planes, height, across = volume.shape
    centers = hat_center.astype(jnp.float32)
    transfer = lax.map(lambda slab_plane: colour(slab_plane.reshape(-1), centers, tf_table), volume)
    transfer = transfer.reshape(planes, 4, height, across)
    shading_term = shading(jnp.pad(volume.astype(jnp.float32), 1))
    opacity = 1.0 - jnp.exp(-transfer[:, 3] * (depth_scale / planes))
    emitted = transfer[:, :3] * shading_term[:, None]
    through = jnp.cumprod(1.0 - opacity, axis=0)
    before = jnp.concatenate([jnp.ones_like(through[:1]), through[:-1]], axis=0)
    colour_sum = lax.optimization_barrier(jnp.sum((before * opacity)[:, None] * emitted, axis=0))
    return jnp.concatenate([colour_sum, 1.0 - through[-1][None]], axis=0)
```

```python
import functools

import jax
import jax.numpy as jnp
from jax import lax
from jax.experimental import pallas as pl
from jax.experimental.pallas import tpu as pltpu
from jax.sharding import PartitionSpec as P

NBIN = 256
HW = 4

ambient = 0.3
grad_floor = 0.01
depth_scale = 1.5

LANES = 128
GROUPS = 7
PHASES = 4
AHEAD = 2
STEPS = 65534.0
FINE = 64.0
MESH = pl.DeviceIdType.MESH
F32 = jnp.float32
I16 = jnp.int16
I32 = jnp.int32
BF16 = jnp.bfloat16


def build_tables(center_ref, table_ref, tab):
    centers = center_ref[...].astype(F32)
    wide = table_ref[...].astype(F32)
    copies = jnp.concatenate(
        [jnp.broadcast_to(wide[c : c + 1], (8, NBIN)) for c in range(4)], axis=0
    ).astype(BF16)
    centers = jnp.broadcast_to(centers, (LANES, NBIN))
    row = lax.broadcasted_iota(jnp.int32, (LANES, NBIN), 0).astype(F32)
    away = centers - row

    def hats(level):
        return jnp.maximum(0.0, 1.0 - jnp.abs(level - centers) / HW)

    groups = [
        hats((row + LANES) * (1.0 / (2 * LANES)) * (NBIN - 1)),
        jnp.where(away == -3.0, 0.0, jnp.maximum(0.0, 1.0 - jnp.abs(away) / HW)),
        jnp.where((away == 1.0) | (away == 2.0), 1.0, jnp.where((away == 0.0) | (away == -1.0), -1.0, 0.0)),
        jnp.where(away == 3.0, 1.0, jnp.where(away == -2.0, -1.0, 0.0)),
        jnp.where(away == 4.0, 1.0, 0.0),
        jnp.where(away == -3.0, 1.0, 0.0),
        hats(jnp.full((LANES, NBIN), float(NBIN - 1), F32)),
    ]
    for group, weights in enumerate(groups):
        tab[:, group * LANES : (group + 1) * LANES] = lax.dot_general(
            copies, weights.astype(BF16), (((1,), (1,)), ((), ())), preferred_element_type=F32
        )


def lookup(values, tab):
    level = values * float(NBIN - 1)
    bin_index = level.astype(jnp.int32)
    part_bin = level - bin_index.astype(F32)
    quarter = part_bin * 0.25
    coarse = (quarter + 1.5 * 2.0**15) - 1.5 * 2.0**15
    fine = (quarter + 1.5 * 2.0**14) - 1.5 * 2.0**14
    rising = quarter.astype(BF16).astype(F32)
    falling = ((1.0 - part_bin) * 0.25).astype(BF16).astype(F32)
    low_index = bin_index & (LANES - 1)
    high_index = (values * float(2 * LANES)).astype(jnp.int32) & (LANES - 1)
    upper, top = values >= 0.5, values >= 1.0

    def entry(c, group):
        return tab[8 * c : 8 * c + 8, group * LANES : (group + 1) * LANES]

    out = []
    for c in range(4):
        flat, per_coarse, per_fine, per_rising, per_falling = (
            jnp.take_along_axis(entry(c, 1 + k), low_index, axis=1) for k in range(5)
        )
        total = (flat + coarse * per_coarse) + (fine * per_fine + rising * per_rising + falling * per_falling)
        out.append(total)
    for c in range(4):
        high = jnp.take_along_axis(entry(c, 0), high_index, axis=1)
        out[c] = jnp.where(top, entry(c, 6), jnp.where(upper, high, out[c]))
    return out


def fold(mine, theirs, i_am_front):
    ahead = jnp.where(i_am_front, mine[3], theirs[3])
    mixed = []
    for c in range(3):
        a = jnp.where(i_am_front, mine[c], theirs[c])
        b = jnp.where(i_am_front, theirs[c], mine[c])
        mixed.append(a + ahead * b)
    mixed.append(mine[3] * theirs[3])
    return mixed


def encode(values, code):
    rows, across = values[0].shape
    row = lax.broadcasted_iota(jnp.int32, (rows, across), 0)
    powers = jnp.zeros((rows, across), I32)
    for c in range(4):
        top = jnp.maximum(jnp.max(values[c], axis=0, keepdims=True), 1e-30)
        power = jnp.floor(jnp.log(top) * (FINE * 1.4426950408889634)) + 2.0
        level = values[c] * (jnp.exp2(power * (-1.0 / FINE)) * STEPS) + 0.5
        code[c] = (jnp.minimum(level, STEPS).astype(I32) - 32767).astype(I16)
        powers = jnp.where(row == c, power.astype(I32), powers)
    code[4] = powers.astype(I16)


def decode(code, c):
    power = code[4].astype(I32).astype(F32)[c : c + 1]
    return (code[c].astype(I32).astype(F32) + 32767.0) * (jnp.exp2(power * (1.0 / FINE)) * (1.0 / STEPS))


def body(sizes, vol_in, center_in, table_in, out, vol, center_ref, table_ref, tab, xsd, look, zhalo, face, faces, rows_out, rows_in, part, recv, code,
         ls, zs, zr, fs, fr, rs, rr, ps, pr, gs, gr, ns, nr):
    nx, ny, nz = sizes
    planes, height, across = vol.shape
    ix, iy, iz = lax.axis_index("gx"), lax.axis_index("gy"), lax.axis_index("gz")
    depth = planes * nz
    bit0, bit1 = iz % 2, iz // 2
    near = iz + 1 - 2 * bit0
    far = iz + 2 - 4 * bit1
    diag = near + 2 - 4 * bit1

    loads = [
        pltpu.make_async_copy(src, dst, ls.at[n])
        for n, (src, dst) in enumerate(((vol_in, vol), (center_in, center_ref), (table_in, table_ref)))
    ]
    for load in loads:
        load.start()

    faces[...] = jnp.zeros_like(faces)
    rows_in[...] = jnp.zeros_like(rows_in)
    barrier = pltpu.get_barrier_semaphore()
    for there in (near, far, diag):
        pl.semaphore_signal(barrier, inc=1, device_id=(ix, iy, there), device_id_type=MESH)
    for t in range(1, nx):
        pl.semaphore_signal(barrier, inc=1, device_id=((ix + t) % nx, iy, iz), device_id_type=MESH)
    count = 2 + nx
    for s in (-1, 1):
        for t in (-1, 0, 1):
            there = (iy + s >= 0) & (iy + s < ny) & (ix + t >= 0) & (ix + t < nx)
            count = count + there.astype(jnp.int32)

            @pl.when(there)
            def _(s=s, t=t):
                pl.semaphore_signal(barrier, inc=1, device_id=(ix + t, iy + s, iz), device_id_type=MESH)

    def remote(src, dst, ssem, rsem, where):
        return pltpu.make_async_remote_copy(
            src_ref=src, dst_ref=dst, send_sem=ssem, recv_sem=rsem, device_id=where, device_id_type=MESH
        )

    front, back = iz > 0, iz < nz - 1
    to_back = remote(vol.at[planes - 1], zhalo.at[0], zs.at[0], zr.at[0], (ix, iy, iz + 1))
    to_front = remote(vol.at[0], zhalo.at[1], zs.at[1], zr.at[1], (ix, iy, iz - 1))

    loads[1].wait()
    loads[2].wait()
    build_tables(center_ref, table_ref, tab)
    loads[0].wait()

    source = lax.broadcasted_iota(jnp.int32, (across, across), 0)
    target = lax.broadcasted_iota(jnp.int32, (across, across), 1)
    gap = source - target
    blur = jnp.where(gap == 0, 2.0, jnp.where(jnp.abs(gap) == 1, 1.0, 0.0))
    slope = jnp.where(gap == 1, 1.0, jnp.where(gap == -1, -1.0, 0.0))
    stencil = jnp.concatenate([blur, slope], axis=1).astype(BF16)

    def edge_columns(cells, plane):
        right = jnp.where((source == across - 1) & (target == 2 * plane + 1), 1.0, 0.0)
        left = jnp.where((source == 0) & (target == 2 * plane), 1.0, 0.0)
        return jnp.dot(cells, (right + left).astype(BF16), preferred_element_type=F32)

    def own_plane(z, acc):
        cells = vol[z]
        xsd[z + 1, pl.ds(8, height), :] = jnp.dot(cells, stencil, preferred_element_type=F32)
        return acc + edge_columns(cells, z + 1)

    pl.semaphore_wait(barrier, count)

    @pl.when(back)
    def _():
        to_back.start()

    @pl.when(front)
    def _():
        to_front.start()

    columns = lax.fori_loop(0, planes, own_plane, jnp.zeros((height, across), F32))

    block = height // (2 * PHASES)

    def start_of(b):
        side = bit0 if b % 2 else 1 - bit0
        return pl.multiple_of((b // 2) * 2 * block + side * block, 16)

    def look_plane(b, z):
        cells = vol[z, pl.ds(start_of(b), block), :].astype(F32)
        for k in range(block // 8):
            four = lookup(cells[8 * k : 8 * k + 8], tab)
            for c in range(4):
                look[b, c, z, 8 * k : 8 * k + 8, :] = four[c]

    def look_block(b):
        def step(n, carry):
            for k in range(4):
                look_plane(b, 4 * n + k)
            return carry

        lax.fori_loop(0, planes // 4, step, 0)

    look_block(0)

    @pl.when(back)
    def _():
        to_back.wait_send()
        to_front.wait_recv()

    @pl.when(front)
    def _():
        to_front.wait_send()
        to_back.wait_recv()

    @pl.when(jnp.logical_not(front))
    def _():
        zhalo[0] = jnp.zeros_like(zhalo[0])

    @pl.when(jnp.logical_not(back))
    def _():
        zhalo[1] = jnp.zeros_like(zhalo[1])

    for slot, plane in ((0, 0), (1, planes + 1)):
        cells = zhalo[slot]
        xsd[plane, pl.ds(8, height), :] = jnp.dot(cells, stencil, preferred_element_type=F32)
        columns = columns + edge_columns(cells, plane)
    face[...] = columns.astype(BF16)

    def edge_rows(row):
        own = vol[:, row, :].astype(F32)
        pad = jnp.zeros((rows_out.shape[1] - planes - 2, across), F32)
        ends = [zhalo[slot, row : row + 1, :].astype(F32) for slot in (0, 1)]
        return jnp.concatenate([ends[0], own, ends[1], pad], axis=0).astype(BF16)

    rows_out[0] = edge_rows(0)
    rows_out[1] = edge_rows(height - 1)

    halo = []
    for s, slot in ((1, 0), (-1, 1)):
        sending = (ix + s >= 0) & (ix + s < nx)
        taking = (ix - s >= 0) & (ix - s < nx)
        halo.append((sending, taking, remote(face, faces.at[slot], fs.at[slot], fr.at[slot], (ix + s, iy, iz))))
    for s, side in ((1, 0), (-1, 1)):
        for t in (-1, 0, 1):
            slot = 1 - t
            sending = (iy + s >= 0) & (iy + s < ny) & (ix + t >= 0) & (ix + t < nx)
            taking = (iy - s >= 0) & (iy - s < ny) & (ix - t >= 0) & (ix - t < nx)
            halo.append(
                (sending, taking, remote(rows_out.at[1 - side], rows_in.at[side, slot], rs.at[side, slot], rr.at[side, slot], (ix + t, iy + s, iz)))
            )
    for sending, _, copy in halo:

        @pl.when(sending)
        def _(copy=copy):
            copy.start()

    for b in range(1, AHEAD):
        look_block(b)

    for sending, taking, copy in halo:

        @pl.when(taking)
        def _(copy=copy):
            copy.wait_recv()

        @pl.when(sending)
        def _(copy=copy):
            copy.wait_send()

    lane = lax.broadcasted_iota(jnp.int32, (height, across), 1)
    both = jnp.where(lane % 2 == 1, faces[0].astype(F32), faces[1].astype(F32))
    ends = jnp.where((lane == 0) | (lane == across - 1), 1.0, 0.0)
    sign = jnp.where(lane == 0, -1.0, jnp.where(lane == across - 1, 1.0, 0.0))

    def add_columns(z, carry):
        placed = pltpu.roll(both, across - 2 * z - 1, 1)
        xsd[z, pl.ds(8, height), :] += jnp.concatenate([placed * ends, placed * sign], axis=1)
        return carry

    lax.fori_loop(0, planes + 2, add_columns, 0)
    count_rows = rows_out.shape[1]
    for side in (0, 1):
        strip = jnp.dot(rows_in[side, 1], stencil, preferred_element_type=F32)
        left = pltpu.roll(rows_in[side, 0].astype(F32), 1, 1)
        right = pltpu.roll(rows_in[side, 2].astype(F32), across - 1, 1)
        short = lax.broadcasted_iota(jnp.int32, (count_rows, across), 1)
        left = jnp.where(short == 0, left, 0.0)
        right = jnp.where(short == across - 1, right, 0.0)
        strip = strip + jnp.concatenate([left + right, right - left], axis=1)
        row = 7 if side == 0 else 8 + height
        for z in range(planes + 2):
            xsd[z, row : row + 1, :] = strip[z : z + 1]

    shade_scale = (1.0 - ambient) / (32.0 * 3.0**0.5)

    sub = lax.broadcasted_iota(jnp.int32, (8, 2 * across), 0)

    def march(b, own):
        row = pl.multiple_of(start_of(b) + own, 8)

        def gradients(z):
            above = xsd[z, pl.ds(row, 8), :]
            mid = xsd[z, pl.ds(row + 8, 8), :]
            below = xsd[z, pl.ds(row + 16, 8), :]
            up = pltpu.roll(jnp.where(sub == 7, above, mid), 1, 0)
            down = pltpu.roll(jnp.where(sub == 0, below, mid), 7, 0)
            smoothed = up + 2.0 * mid + down
            return smoothed[:, across:], down[:, :across] - up[:, :across], smoothed[:, :across]

        through = jnp.ones((8, across), F32)
        sums = [jnp.zeros((8, across), F32) for _ in range(3)]
        before, here = gradients(0), gradients(1)
        for z in range(planes):
            after = gradients(z + 2)
            grad_x = before[0] + 2.0 * here[0] + after[0]
            grad_y = before[1] + 2.0 * here[1] + after[1]
            grad_z = after[2] - before[2]
            before, here = here, after
            square = (grad_x * grad_x + grad_y * grad_y + grad_z * grad_z) * (1.0 / 1024.0) + grad_floor
            shade = ambient + shade_scale * jnp.abs(grad_x + grad_y + grad_z) * lax.rsqrt(square)
            clear = jnp.exp(look[b, 3, z, pl.ds(own, 8), :] * (-depth_scale / depth))
            weight = through * (1.0 - clear) * shade
            for c in range(3):
                sums[c] = sums[c] + weight * look[b, c, z, pl.ds(own, 8), :]
            through = through * clear
        for c in range(3):
            part[b, c, pl.ds(own, 8), :] = sums[c]
        part[b, 3, pl.ds(own, 8), :] = through

    groups = block // 8
    share = planes // groups

    def render(b):
        def step(n, carry):
            march(b, pl.multiple_of(8 * n, 8))
            if b + AHEAD < 2 * PHASES:
                for k in range(share):
                    look_plane(b + AHEAD, share * n + k)
            return carry

        lax.fori_loop(0, groups, step, 0)

    def to_near(p):
        return remote(part.at[2 * p], recv.at[p, 0], ps.at[p, 0], pr.at[p, 0], (ix, iy, near))

    def to_far(p):
        return remote(part.at[2 * p + 1], recv.at[p, 1], ps.at[p, 1], pr.at[p, 1], (ix, iy, far))

    def to_diag(p):
        return remote(part.at[2 * p], recv.at[p, 2], ps.at[p, 2], pr.at[p, 2], (ix, iy, diag))

    def along(p, t):
        tile = code.at[p, bit0, ix]
        return remote(tile, tile, gs.at[p, t - 1], gr.at[p, t - 1], ((ix + t) % nx, iy, iz))

    def hand(p):
        half = code.at[p, bit0]
        return remote(half, half, ns.at[p], nr.at[p], (ix, iy, near))

    def composite(p):
        for copy in (to_near(p), to_diag(p), to_far(p)):
            copy.wait_recv()
        mine = fold([part[2 * p + 1, c] for c in range(4)], [recv[p, 0, c] for c in range(4)], bit0 == 0)
        others = fold([recv[p, 1, c] for c in range(4)], [recv[p, 2, c] for c in range(4)], bit0 == 0)
        quad = fold(mine, others, bit1 == 0)
        quad[3] = 1.0 - quad[3]
        encode(quad, code.at[p, bit0, ix])
        for t in range(nx - 1, 0, -1):
            along(p, t).start()

    def show(p, side):
        rows = pl.ds(pl.multiple_of(p * 2 * block + side * block, 16), block)
        for j in range(nx):
            for c in range(4):
                out[c, rows, j * across : (j + 1) * across] = decode(code.at[p, side, j], c)

    def pass_on(p):
        for t in range(1, nx):
            along(p, t).wait_recv()
        hand(p).start()

    def take(p):
        half = code.at[p, 1 - bit0]
        remote(half, half, ns.at[p], nr.at[p], (ix, iy, near)).wait_recv()
        show(p, 1 - bit0)

    for b in range(2 * PHASES):
        render(b)
        p = b // 2
        if b % 2 == 0:
            to_diag(p).start()
            to_near(p).start()
            if p >= 1:
                composite(p - 1)
        else:
            to_far(p).start()
            if p >= 2:
                pass_on(p - 2)
                show(p - 2, bit0)
    last = PHASES - 1
    for p in range(max(PHASES - 2, 0)):
        take(p)
    composite(last)
    for p in range(max(PHASES - 2, 0), PHASES):
        pass_on(p)
        show(p, bit0)
        take(p)

    for p in range(PHASES):
        for copy in (to_near(p), to_diag(p), to_far(p), hand(p)):
            copy.wait_send()
        for t in range(1, nx):
            along(p, t).wait_send()


def shards(volume, hat_center, tf_table):
    planes, height, across = volume.shape
    sizes = tuple(lax.axis_size(a) for a in ("gx", "gy", "gz"))
    nx = sizes[0]
    assert sizes[2] == 4 and across == LANES and height % (32 * PHASES) == 0
    extended_rows = -(-(planes + 2) // 16) * 16
    block = height // (2 * PHASES)
    dma = pltpu.SemaphoreType.DMA
    vmem = pl.BlockSpec(memory_space=pltpu.VMEM)
    hbm = pl.BlockSpec(memory_space=pltpu.MemorySpace.HBM)
    return pl.pallas_call(
        functools.partial(body, sizes),
        out_shape=jax.ShapeDtypeStruct((4, height, across * nx), F32),
        in_specs=[hbm] * 3,
        out_specs=vmem,
        scratch_shapes=[
            pltpu.VMEM((planes, height, across), BF16),
            pltpu.VMEM((1, NBIN), I32),
            pltpu.VMEM((4, NBIN), BF16),
            pltpu.VMEM((32, GROUPS * LANES), F32),
            pltpu.VMEM((planes + 2, height + 16, 2 * across), F32),
            pltpu.VMEM((2 * PHASES, 4, planes, block, across), F32),
            pltpu.VMEM((2, height, across), BF16),
            pltpu.VMEM((height, across), BF16),
            pltpu.VMEM((2, height, across), BF16),
            pltpu.VMEM((2, extended_rows, across), BF16),
            pltpu.VMEM((2, 3, extended_rows, across), BF16),
            pltpu.VMEM((2 * PHASES, 4, block, across), F32),
            pltpu.VMEM((PHASES, 3, 4, block, across), F32),
            pltpu.VMEM((PHASES, 2, nx, 5, block, across), I16),
            dma((3,)),
            dma((2,)), dma((2,)),
            dma((2,)), dma((2,)),
            dma((2, 3)), dma((2, 3)),
            dma((PHASES, 3)), dma((PHASES, 3)),
            dma((PHASES, nx)), dma((PHASES, nx)),
            dma((PHASES,)), dma((PHASES,)),
        ],
        compiler_params=pltpu.CompilerParams(collective_id=0, has_side_effects=True, vmem_limit_bytes=48 << 20),
    )(volume, hat_center.reshape(1, -1), tf_table)


def solution(mesh):
    in_specs = (P("gz", "gy", "gx"), P(), P())
    out_specs = P(None, "gy", None)
    return jax.shard_map(shards, mesh=mesh, in_specs=in_specs, out_specs=out_specs, check_vma=False)
```

```python
import functools

import jax
import jax.numpy as jnp
from jax import lax
from jax.experimental import pallas as pl
from jax.experimental.pallas import tpu as pltpu
from jax.sharding import PartitionSpec as P

NBIN = 256
HW = 4

ambient = 0.3
grad_floor = 0.01
depth_scale = 1.5

LANES = 128
GROUPS = 7
PHASES = 4
BEFORE, MIDDLE, AFTER = 2, 1, 2
AHEAD = BEFORE + MIDDLE + AFTER
STEPS = 65534.0
FINE = 64.0
MESH = pl.DeviceIdType.MESH
F32 = jnp.float32
I16 = jnp.int16
I32 = jnp.int32
BF16 = jnp.bfloat16


def build_tables(center_ref, table_ref, tab):
    centers = center_ref[...].astype(F32)
    wide = table_ref[...].astype(F32)
    copies = jnp.concatenate(
        [jnp.broadcast_to(wide[c : c + 1], (8, NBIN)) for c in range(4)], axis=0
    ).astype(BF16)
    centers = jnp.broadcast_to(centers, (LANES, NBIN))
    row = lax.broadcasted_iota(jnp.int32, (LANES, NBIN), 0).astype(F32)
    away = centers - row

    def hats(level):
        return jnp.maximum(0.0, 1.0 - jnp.abs(level - centers) / HW)

    groups = [
        hats((row + LANES) * (1.0 / (2 * LANES)) * (NBIN - 1)),
        jnp.where(away == -3.0, 0.0, jnp.maximum(0.0, 1.0 - jnp.abs(away) / HW)),
        jnp.where((away == 1.0) | (away == 2.0), 1.0, jnp.where((away == 0.0) | (away == -1.0), -1.0, 0.0)),
        jnp.where(away == 3.0, 1.0, jnp.where(away == -2.0, -1.0, 0.0)),
        jnp.where(away == 4.0, 1.0, 0.0),
        jnp.where(away == -3.0, 1.0, 0.0),
        hats(jnp.full((LANES, NBIN), float(NBIN - 1), F32)),
    ]
    for group, weights in enumerate(groups):
        tab[:, group * LANES : (group + 1) * LANES] = lax.dot_general(
            copies, weights.astype(BF16), (((1,), (1,)), ((), ())), preferred_element_type=F32
        )


def lookup(values, tab):
    level = values * float(NBIN - 1)
    bin_index = level.astype(jnp.int32)
    part_bin = level - bin_index.astype(F32)
    quarter = part_bin * 0.25
    coarse = (quarter + 1.5 * 2.0**15) - 1.5 * 2.0**15
    fine = (quarter + 1.5 * 2.0**14) - 1.5 * 2.0**14
    rising = quarter.astype(BF16).astype(F32)
    falling = ((1.0 - part_bin) * 0.25).astype(BF16).astype(F32)
    low_index = bin_index & (LANES - 1)
    high_index = (values * float(2 * LANES)).astype(jnp.int32) & (LANES - 1)
    upper, top = values >= 0.5, values >= 1.0

    def entry(c, group):
        return tab[8 * c : 8 * c + 8, group * LANES : (group + 1) * LANES]

    out = []
    for c in range(4):
        flat, per_coarse, per_fine, per_rising, per_falling = (
            jnp.take_along_axis(entry(c, 1 + k), low_index, axis=1) for k in range(5)
        )
        total = (flat + coarse * per_coarse) + (fine * per_fine + rising * per_rising + falling * per_falling)
        out.append(total)
    for c in range(4):
        high = jnp.take_along_axis(entry(c, 0), high_index, axis=1)
        out[c] = jnp.where(top, entry(c, 6), jnp.where(upper, high, out[c]))
    return out


def fold(mine, theirs, i_am_front):
    ahead = jnp.where(i_am_front, mine[3], theirs[3])
    mixed = []
    for c in range(3):
        a = jnp.where(i_am_front, mine[c], theirs[c])
        b = jnp.where(i_am_front, theirs[c], mine[c])
        mixed.append(a + ahead * b)
    mixed.append(mine[3] * theirs[3])
    return mixed


def encode(values, code):
    rows, across = values[0].shape
    row = lax.broadcasted_iota(jnp.int32, (rows, across), 0)
    powers = jnp.zeros((rows, across), I32)
    for c in range(4):
        top = jnp.maximum(jnp.max(values[c], axis=0, keepdims=True), 1e-30)
        power = jnp.floor(jnp.log(top) * (FINE * 1.4426950408889634)) + 2.0
        level = values[c] * (jnp.exp2(power * (-1.0 / FINE)) * STEPS) + 0.5
        code[c] = (jnp.minimum(level, STEPS).astype(I32) - 32767).astype(I16)
        powers = jnp.where(row == c, power.astype(I32), powers)
    code[4] = powers.astype(I16)


def decode(code, c):
    power = code[4].astype(I32).astype(F32)[c : c + 1]
    return (code[c].astype(I32).astype(F32) + 32767.0) * (jnp.exp2(power * (1.0 / FINE)) * (1.0 / STEPS))


def body(sizes, vol_in, center_in, table_in, out, vol, center_ref, table_ref, tab, xsd, look, zhalo, face, faces, rows_out, rows_in, part, pair, recv, code,
         ls, zs, zr, fs, fr, rs, rr, ps, pr, gs, gr, ns, nr):
    nx, ny, nz = sizes
    planes, height, across = vol.shape
    ix, iy, iz = lax.axis_index("gx"), lax.axis_index("gy"), lax.axis_index("gz")
    depth = planes * nz
    bit0, bit1 = iz % 2, iz // 2
    near = iz + 1 - 2 * bit0
    far = iz + 2 - 4 * bit1
    diag = near + 2 - 4 * bit1

    loads = [
        pltpu.make_async_copy(src, dst, ls.at[n])
        for n, (src, dst) in enumerate(((vol_in, vol), (center_in, center_ref), (table_in, table_ref)))
    ]
    for load in loads:
        load.start()

    faces[...] = jnp.zeros_like(faces)
    rows_in[...] = jnp.zeros_like(rows_in)
    barrier = pltpu.get_barrier_semaphore()
    for there in (near, far, diag):
        pl.semaphore_signal(barrier, inc=1, device_id=(ix, iy, there), device_id_type=MESH)
    for t in range(1, nx):
        pl.semaphore_signal(barrier, inc=1, device_id=((ix + t) % nx, iy, iz), device_id_type=MESH)
    count = 2 + nx
    for s in (-1, 1):
        for t in (-1, 0, 1):
            there = (iy + s >= 0) & (iy + s < ny) & (ix + t >= 0) & (ix + t < nx)
            count = count + there.astype(jnp.int32)

            @pl.when(there)
            def _(s=s, t=t):
                pl.semaphore_signal(barrier, inc=1, device_id=(ix + t, iy + s, iz), device_id_type=MESH)

    def remote(src, dst, ssem, rsem, where):
        return pltpu.make_async_remote_copy(
            src_ref=src, dst_ref=dst, send_sem=ssem, recv_sem=rsem, device_id=where, device_id_type=MESH
        )

    front, back = iz > 0, iz < nz - 1
    to_back = remote(vol.at[planes - 1], zhalo.at[0], zs.at[0], zr.at[0], (ix, iy, iz + 1))
    to_front = remote(vol.at[0], zhalo.at[1], zs.at[1], zr.at[1], (ix, iy, iz - 1))

    loads[1].wait()
    loads[2].wait()
    build_tables(center_ref, table_ref, tab)
    loads[0].wait()

    source = lax.broadcasted_iota(jnp.int32, (across, across), 0)
    target = lax.broadcasted_iota(jnp.int32, (across, across), 1)
    gap = source - target
    blur = jnp.where(gap == 0, 2.0, jnp.where(jnp.abs(gap) == 1, 1.0, 0.0))
    slope = jnp.where(gap == 1, 1.0, jnp.where(gap == -1, -1.0, 0.0))
    stencil = jnp.concatenate([blur, slope], axis=1).astype(BF16)

    def edge_columns(cells, plane):
        right = jnp.where((source == across - 1) & (target == 2 * plane + 1), 1.0, 0.0)
        left = jnp.where((source == 0) & (target == 2 * plane), 1.0, 0.0)
        return jnp.dot(cells, (right + left).astype(BF16), preferred_element_type=F32)

    def own_plane(z, acc):
        cells = vol[z]
        xsd[z + 1, pl.ds(8, height), :] = jnp.dot(cells, stencil, preferred_element_type=F32)
        return acc + edge_columns(cells, z + 1)

    def own_planes(n, acc):
        for k in range(4):
            acc = own_plane(4 * n + k, acc)
        return acc

    block = height // (2 * PHASES)

    def start_of(b):
        side = bit0 if b % 2 else 1 - bit0
        return pl.multiple_of((b // 2) * 2 * block + side * block, 16)

    def look_plane(b, z):
        cells = vol[z, pl.ds(start_of(b), block), :].astype(F32)
        for k in range(block // 8):
            four = lookup(cells[8 * k : 8 * k + 8], tab)
            for c in range(4):
                look[b, c, z, 8 * k : 8 * k + 8, :] = four[c]

    def look_block(b):
        def step(n, carry):
            for k in range(4):
                look_plane(b, 4 * n + k)
            return carry

        lax.fori_loop(0, planes // 4, step, 0)

    for b in range(BEFORE):
        look_block(b)

    pl.semaphore_wait(barrier, count)

    @pl.when(back)
    def _():
        to_back.start()

    @pl.when(front)
    def _():
        to_front.start()

    columns = lax.fori_loop(0, planes // 4, own_planes, jnp.zeros((height, across), F32))

    for b in range(BEFORE, BEFORE + MIDDLE):
        look_block(b)

    @pl.when(back)
    def _():
        to_back.wait_send()
        to_front.wait_recv()

    @pl.when(front)
    def _():
        to_front.wait_send()
        to_back.wait_recv()

    @pl.when(jnp.logical_not(front))
    def _():
        zhalo[0] = jnp.zeros_like(zhalo[0])

    @pl.when(jnp.logical_not(back))
    def _():
        zhalo[1] = jnp.zeros_like(zhalo[1])

    for slot, plane in ((0, 0), (1, planes + 1)):
        cells = zhalo[slot]
        xsd[plane, pl.ds(8, height), :] = jnp.dot(cells, stencil, preferred_element_type=F32)
        columns = columns + edge_columns(cells, plane)
    face[...] = columns.astype(BF16)

    def edge_rows(row):
        own = vol[:, row, :].astype(F32)
        pad = jnp.zeros((rows_out.shape[1] - planes - 2, across), F32)
        ends = [zhalo[slot, row : row + 1, :].astype(F32) for slot in (0, 1)]
        return jnp.concatenate([ends[0], own, ends[1], pad], axis=0).astype(BF16)

    rows_out[0] = edge_rows(0)
    rows_out[1] = edge_rows(height - 1)

    halo = []
    for s, slot in ((1, 0), (-1, 1)):
        sending = (ix + s >= 0) & (ix + s < nx)
        taking = (ix - s >= 0) & (ix - s < nx)
        halo.append((sending, taking, remote(face, faces.at[slot], fs.at[slot], fr.at[slot], (ix + s, iy, iz))))
    for s, side in ((1, 0), (-1, 1)):
        for t in (-1, 0, 1):
            slot = 1 - t
            sending = (iy + s >= 0) & (iy + s < ny) & (ix + t >= 0) & (ix + t < nx)
            taking = (iy - s >= 0) & (iy - s < ny) & (ix - t >= 0) & (ix - t < nx)
            halo.append(
                (sending, taking, remote(rows_out.at[1 - side], rows_in.at[side, slot], rs.at[side, slot], rr.at[side, slot], (ix + t, iy + s, iz)))
            )
    for sending, _, copy in halo:

        @pl.when(sending)
        def _(copy=copy):
            copy.start()

    for b in range(BEFORE + MIDDLE, AHEAD):
        look_block(b)

    for sending, taking, copy in halo:

        @pl.when(taking)
        def _(copy=copy):
            copy.wait_recv()

        @pl.when(sending)
        def _(copy=copy):
            copy.wait_send()

    lane = lax.broadcasted_iota(jnp.int32, (height, across), 1)
    both = jnp.where(lane % 2 == 1, faces[0].astype(F32), faces[1].astype(F32))
    ends = jnp.where((lane == 0) | (lane == across - 1), 1.0, 0.0)
    sign = jnp.where(lane == 0, -1.0, jnp.where(lane == across - 1, 1.0, 0.0))

    def add_columns(z, carry):
        placed = pltpu.roll(both, across - 2 * z - 1, 1)
        xsd[z, pl.ds(8, height), :] += jnp.concatenate([placed * ends, placed * sign], axis=1)
        return carry

    lax.fori_loop(0, planes + 2, add_columns, 0)
    count_rows = rows_out.shape[1]
    for side in (0, 1):
        strip = jnp.dot(rows_in[side, 1], stencil, preferred_element_type=F32)
        left = pltpu.roll(rows_in[side, 0].astype(F32), 1, 1)
        right = pltpu.roll(rows_in[side, 2].astype(F32), across - 1, 1)
        short = lax.broadcasted_iota(jnp.int32, (count_rows, across), 1)
        left = jnp.where(short == 0, left, 0.0)
        right = jnp.where(short == across - 1, right, 0.0)
        strip = strip + jnp.concatenate([left + right, right - left], axis=1)
        row = 7 if side == 0 else 8 + height
        for z in range(planes + 2):
            xsd[z, row : row + 1, :] = strip[z : z + 1]

    shade_scale = (1.0 - ambient) / (32.0 * 3.0**0.5)

    sub = lax.broadcasted_iota(jnp.int32, (8, 2 * across), 0)

    def march(b, own):
        row = pl.multiple_of(start_of(b) + own, 8)

        def gradients(z):
            above = xsd[z, pl.ds(row, 8), :]
            mid = xsd[z, pl.ds(row + 8, 8), :]
            below = xsd[z, pl.ds(row + 16, 8), :]
            up = pltpu.roll(jnp.where(sub == 7, above, mid), 1, 0)
            down = pltpu.roll(jnp.where(sub == 0, below, mid), 7, 0)
            smoothed = up + 2.0 * mid + down
            return smoothed[:, across:], down[:, :across] - up[:, :across], smoothed[:, :across]

        through = jnp.ones((8, across), F32)
        sums = [jnp.zeros((8, across), F32) for _ in range(3)]
        before, here = gradients(0), gradients(1)
        for z in range(planes):
            after = gradients(z + 2)
            grad_x = before[0] + 2.0 * here[0] + after[0]
            grad_y = before[1] + 2.0 * here[1] + after[1]
            grad_z = after[2] - before[2]
            before, here = here, after
            square = (grad_x * grad_x + grad_y * grad_y + grad_z * grad_z) * (1.0 / 1024.0) + grad_floor
            shade = ambient + shade_scale * jnp.abs(grad_x + grad_y + grad_z) * lax.rsqrt(square)
            clear = jnp.exp(look[b, 3, z, pl.ds(own, 8), :] * (-depth_scale / depth))
            weight = through * (1.0 - clear) * shade
            for c in range(3):
                sums[c] = sums[c] + weight * look[b, c, z, pl.ds(own, 8), :]
            through = through * clear
        for c in range(3):
            part[b, c, pl.ds(own, 8), :] = sums[c]
        part[b, 3, pl.ds(own, 8), :] = through

    groups = block // 8
    share = planes // groups

    def render(b):
        def step(n, carry):
            march(b, pl.multiple_of(8 * n, 8))
            if b + AHEAD < 2 * PHASES:
                for k in range(share):
                    look_plane(b + AHEAD, share * n + k)
            return carry

        lax.fori_loop(0, groups, step, 0)

    def to_near(p):
        return remote(part.at[2 * p], recv.at[p, 0], ps.at[p, 0], pr.at[p, 0], (ix, iy, near))

    def to_far(p):
        return remote(pair.at[p], recv.at[p, 1], ps.at[p, 1], pr.at[p, 1], (ix, iy, far))

    def along(p, t):
        tile = code.at[p, bit0, ix]
        return remote(tile, tile, gs.at[p, t - 1], gr.at[p, t - 1], ((ix + t) % nx, iy, iz))

    def hand(p):
        half = code.at[p, bit0]
        return remote(half, half, ns.at[p], nr.at[p], (ix, iy, near))

    def couple(p):
        to_near(p).wait_recv()
        mixed = fold([part[2 * p + 1, c] for c in range(4)], [recv[p, 0, c] for c in range(4)], bit0 == 0)
        for c in range(4):
            pair[p, c] = mixed[c]
        to_far(p).start()

    def composite(p):
        to_far(p).wait_recv()
        quad = fold([pair[p, c] for c in range(4)], [recv[p, 1, c] for c in range(4)], bit1 == 0)
        quad[3] = 1.0 - quad[3]
        encode(quad, code.at[p, bit0, ix])
        for t in range(nx - 1, 0, -1):
            along(p, t).start()

    def show(p, side):
        rows = pl.ds(pl.multiple_of(p * 2 * block + side * block, 16), block)
        for j in range(nx):
            for c in range(4):
                out[c, rows, j * across : (j + 1) * across] = decode(code.at[p, side, j], c)

    def pass_on(p):
        for t in range(1, nx):
            along(p, t).wait_recv()
        hand(p).start()

    def take(p):
        half = code.at[p, 1 - bit0]
        remote(half, half, ns.at[p], nr.at[p], (ix, iy, near)).wait_recv()
        show(p, 1 - bit0)

    def leave(p):
        pass_on(p)
        show(p, bit0)

    last = PHASES - 1
    for b in range(2 * PHASES):
        render(b)
        p = b // 2
        if b % 2 == 0:
            to_near(p).start()
        else:
            couple(p)
    for p in range(PHASES):
        composite(p)
    leave(0)
    for p in range(1, PHASES):
        take(p - 1)
        leave(p)
    take(last)

    for p in range(PHASES):
        for copy in (to_near(p), to_far(p), hand(p)):
            copy.wait_send()
        for t in range(1, nx):
            along(p, t).wait_send()


def shards(volume, hat_center, tf_table):
    planes, height, across = volume.shape
    sizes = tuple(lax.axis_size(a) for a in ("gx", "gy", "gz"))
    nx = sizes[0]
    assert sizes[2] == 4 and across == LANES and height % (32 * PHASES) == 0
    extended_rows = -(-(planes + 2) // 16) * 16
    block = height // (2 * PHASES)
    dma = pltpu.SemaphoreType.DMA
    vmem = pl.BlockSpec(memory_space=pltpu.VMEM)
    hbm = pl.BlockSpec(memory_space=pltpu.MemorySpace.HBM)
    return pl.pallas_call(
        functools.partial(body, sizes),
        out_shape=jax.ShapeDtypeStruct((4, height, across * nx), F32),
        in_specs=[hbm] * 3,
        out_specs=vmem,
        scratch_shapes=[
            pltpu.VMEM((planes, height, across), BF16),
            pltpu.VMEM((1, NBIN), I32),
            pltpu.VMEM((4, NBIN), BF16),
            pltpu.VMEM((32, GROUPS * LANES), F32),
            pltpu.VMEM((planes + 2, height + 16, 2 * across), F32),
            pltpu.VMEM((2 * PHASES, 4, planes, block, across), F32),
            pltpu.VMEM((2, height, across), BF16),
            pltpu.VMEM((height, across), BF16),
            pltpu.VMEM((2, height, across), BF16),
            pltpu.VMEM((2, extended_rows, across), BF16),
            pltpu.VMEM((2, 3, extended_rows, across), BF16),
            pltpu.VMEM((2 * PHASES, 4, block, across), F32),
            pltpu.VMEM((PHASES, 4, block, across), F32),
            pltpu.VMEM((PHASES, 2, 4, block, across), F32),
            pltpu.VMEM((PHASES, 2, nx, 5, block, across), I16),
            dma((3,)),
            dma((2,)), dma((2,)),
            dma((2,)), dma((2,)),
            dma((2, 3)), dma((2, 3)),
            dma((PHASES, 2)), dma((PHASES, 2)),
            dma((PHASES, nx)), dma((PHASES, nx)),
            dma((PHASES,)), dma((PHASES,)),
        ],
        compiler_params=pltpu.CompilerParams(collective_id=0, has_side_effects=True, vmem_limit_bytes=48 << 20),
    )(volume, hat_center.reshape(1, -1), tf_table)


def solution(mesh):
    in_specs = (P("gz", "gy", "gx"), P(), P())
    out_specs = P(None, "gy", None)
    return jax.shard_map(shards, mesh=mesh, in_specs=in_specs, out_specs=out_specs, check_vma=False)
```

```python
import functools

import jax
import jax.numpy as jnp
from jax import lax
from jax.experimental import pallas as pl
from jax.experimental.pallas import tpu as pltpu
from jax.sharding import PartitionSpec as P

NBIN = 256
HW = 4

ambient = 0.3
grad_floor = 0.01
depth_scale = 1.5

LANES = 128
GROUPS = 7
PHASES = 4
BEFORE, MIDDLE, AFTER = 2, 1, 2
AHEAD = BEFORE + MIDDLE + AFTER
STEPS = 65534.0
FINE = 64.0
MESH = pl.DeviceIdType.MESH
F32 = jnp.float32
I16 = jnp.int16
I32 = jnp.int32
BF16 = jnp.bfloat16


def build_tables(center_ref, table_ref, tab):
    centers = center_ref[...].astype(F32)
    wide = table_ref[...].astype(F32)
    copies = jnp.concatenate(
        [jnp.broadcast_to(wide[c : c + 1], (8, NBIN)) for c in range(4)], axis=0
    ).astype(BF16)
    centers = jnp.broadcast_to(centers, (LANES, NBIN))
    row = lax.broadcasted_iota(jnp.int32, (LANES, NBIN), 0).astype(F32)
    away = centers - row

    def hats(level):
        return jnp.maximum(0.0, 1.0 - jnp.abs(level - centers) / HW)

    groups = [
        hats((row + LANES) * (1.0 / (2 * LANES)) * (NBIN - 1)),
        jnp.where(away == -3.0, 0.0, jnp.maximum(0.0, 1.0 - jnp.abs(away) / HW)),
        jnp.where((away == 1.0) | (away == 2.0), 1.0, jnp.where((away == 0.0) | (away == -1.0), -1.0, 0.0)),
        jnp.where(away == 3.0, 1.0, jnp.where(away == -2.0, -1.0, 0.0)),
        jnp.where(away == 4.0, 1.0, 0.0),
        jnp.where(away == -3.0, 1.0, 0.0),
        hats(jnp.full((LANES, NBIN), float(NBIN - 1), F32)),
    ]
    for group, weights in enumerate(groups):
        tab[:, group * LANES : (group + 1) * LANES] = lax.dot_general(
            copies, weights.astype(BF16), (((1,), (1,)), ((), ())), preferred_element_type=F32
        )


def lookup(values, tab):
    level = values * float(NBIN - 1)
    bin_index = level.astype(jnp.int32)
    part_bin = level - bin_index.astype(F32)
    quarter = part_bin * 0.25
    coarse = (quarter + 1.5 * 2.0**15) - 1.5 * 2.0**15
    fine = (quarter + 1.5 * 2.0**14) - 1.5 * 2.0**14
    rising = quarter.astype(BF16).astype(F32)
    falling = ((1.0 - part_bin) * 0.25).astype(BF16).astype(F32)
    low_index = bin_index & (LANES - 1)
    high_index = (values * float(2 * LANES)).astype(jnp.int32) & (LANES - 1)
    upper, top = values >= 0.5, values >= 1.0

    def entry(c, group):
        return tab[8 * c : 8 * c + 8, group * LANES : (group + 1) * LANES]

    out = []
    for c in range(4):
        flat, per_coarse, per_fine, per_rising, per_falling = (
            jnp.take_along_axis(entry(c, 1 + k), low_index, axis=1) for k in range(5)
        )
        total = (flat + coarse * per_coarse) + (fine * per_fine + rising * per_rising + falling * per_falling)
        out.append(total)
    for c in range(4):
        high = jnp.take_along_axis(entry(c, 0), high_index, axis=1)
        out[c] = jnp.where(top, entry(c, 6), jnp.where(upper, high, out[c]))
    return out


def fold(mine, theirs, i_am_front):
    ahead = jnp.where(i_am_front, mine[3], theirs[3])
    mixed = []
    for c in range(3):
        a = jnp.where(i_am_front, mine[c], theirs[c])
        b = jnp.where(i_am_front, theirs[c], mine[c])
        mixed.append(a + ahead * b)
    mixed.append(mine[3] * theirs[3])
    return mixed


def encode(values, code):
    rows, across = values[0].shape
    row = lax.broadcasted_iota(jnp.int32, (rows, across), 0)
    powers = jnp.zeros((rows, across), I32)
    for c in range(4):
        top = jnp.maximum(jnp.max(values[c], axis=0, keepdims=True), 1e-30)
        power = jnp.floor(jnp.log(top) * (FINE * 1.4426950408889634)) + 2.0
        level = values[c] * (jnp.exp2(power * (-1.0 / FINE)) * STEPS) + 0.5
        code[c] = (jnp.minimum(level, STEPS).astype(I32) - 32767).astype(I16)
        powers = jnp.where(row == c, power.astype(I32), powers)
    code[4] = powers.astype(I16)


def decode(code, c):
    power = code[4].astype(I32).astype(F32)[c : c + 1]
    return (code[c].astype(I32).astype(F32) + 32767.0) * (jnp.exp2(power * (1.0 / FINE)) * (1.0 / STEPS))


def body(sizes, vol_in, center_in, table_in, out, vol, center_ref, table_ref, tab, xsd, look, zhalo, face, faces, rows_out, rows_in, part, pair, recv, code,
         ls, zs, zr, fs, fr, rs, rr, ps, pr, gs, gr, ns, nr):
    nx, ny, nz = sizes
    planes, height, across = vol.shape
    ix, iy, iz = lax.axis_index("gx"), lax.axis_index("gy"), lax.axis_index("gz")
    depth = planes * nz
    bit0, bit1 = iz % 2, iz // 2
    near = iz + 1 - 2 * bit0
    far = iz + 2 - 4 * bit1
    diag = near + 2 - 4 * bit1

    loads = [
        pltpu.make_async_copy(src, dst, ls.at[n])
        for n, (src, dst) in enumerate(((vol_in, vol), (center_in, center_ref), (table_in, table_ref)))
    ]
    for load in loads:
        load.start()

    faces[...] = jnp.zeros_like(faces)
    rows_in[...] = jnp.zeros_like(rows_in)
    barrier = pltpu.get_barrier_semaphore()
    for there in (near, far, diag):
        pl.semaphore_signal(barrier, inc=1, device_id=(ix, iy, there), device_id_type=MESH)
    for t in range(1, nx):
        pl.semaphore_signal(barrier, inc=1, device_id=((ix + t) % nx, iy, iz), device_id_type=MESH)
    count = 2 + nx
    for s in (-1, 1):
        for t in (-1, 0, 1):
            there = (iy + s >= 0) & (iy + s < ny) & (ix + t >= 0) & (ix + t < nx)
            count = count + there.astype(jnp.int32)

            @pl.when(there)
            def _(s=s, t=t):
                pl.semaphore_signal(barrier, inc=1, device_id=(ix + t, iy + s, iz), device_id_type=MESH)

    def remote(src, dst, ssem, rsem, where):
        return pltpu.make_async_remote_copy(
            src_ref=src, dst_ref=dst, send_sem=ssem, recv_sem=rsem, device_id=where, device_id_type=MESH
        )

    front, back = iz > 0, iz < nz - 1
    to_back = remote(vol.at[planes - 1], zhalo.at[0], zs.at[0], zr.at[0], (ix, iy, iz + 1))
    to_front = remote(vol.at[0], zhalo.at[1], zs.at[1], zr.at[1], (ix, iy, iz - 1))

    loads[1].wait()
    loads[2].wait()
    build_tables(center_ref, table_ref, tab)
    loads[0].wait()

    source = lax.broadcasted_iota(jnp.int32, (across, across), 0)
    target = lax.broadcasted_iota(jnp.int32, (across, across), 1)
    gap = source - target
    blur = jnp.where(gap == 0, 2.0, jnp.where(jnp.abs(gap) == 1, 1.0, 0.0))
    slope = jnp.where(gap == 1, 1.0, jnp.where(gap == -1, -1.0, 0.0))
    stencil = jnp.concatenate([blur, slope], axis=1).astype(BF16)

    def edge_columns(cells, plane):
        right = jnp.where((source == across - 1) & (target == 2 * plane + 1), 1.0, 0.0)
        left = jnp.where((source == 0) & (target == 2 * plane), 1.0, 0.0)
        return jnp.dot(cells, (right + left).astype(BF16), preferred_element_type=F32)

    def own_plane(z, acc):
        cells = vol[z]
        xsd[z + 1, pl.ds(8, height), :] = jnp.dot(cells, stencil, preferred_element_type=F32)
        return acc + edge_columns(cells, z + 1)

    def own_planes(n, acc):
        for k in range(4):
            acc = own_plane(4 * n + k, acc)
        return acc

    block = height // (2 * PHASES)

    def start_of(b):
        side = bit0 if b % 2 else 1 - bit0
        return pl.multiple_of((b // 2) * 2 * block + side * block, 16)

    def look_plane(b, z):
        cells = vol[z, pl.ds(start_of(b), block), :].astype(F32)
        for k in range(block // 8):
            four = lookup(cells[8 * k : 8 * k + 8], tab)
            for c in range(4):
                look[b, c, z, 8 * k : 8 * k + 8, :] = four[c]

    def look_block(b):
        def step(n, carry):
            for k in range(4):
                look_plane(b, 4 * n + k)
            return carry

        lax.fori_loop(0, planes // 4, step, 0)

    for b in range(BEFORE):
        look_block(b)

    pl.semaphore_wait(barrier, count)

    @pl.when(back)
    def _():
        to_back.start()

    @pl.when(front)
    def _():
        to_front.start()

    columns = lax.fori_loop(0, planes // 4, own_planes, jnp.zeros((height, across), F32))

    for b in range(BEFORE, BEFORE + MIDDLE):
        look_block(b)

    @pl.when(back)
    def _():
        to_back.wait_send()
        to_front.wait_recv()

    @pl.when(front)
    def _():
        to_front.wait_send()
        to_back.wait_recv()

    @pl.when(jnp.logical_not(front))
    def _():
        zhalo[0] = jnp.zeros_like(zhalo[0])

    @pl.when(jnp.logical_not(back))
    def _():
        zhalo[1] = jnp.zeros_like(zhalo[1])

    for slot, plane in ((0, 0), (1, planes + 1)):
        cells = zhalo[slot]
        xsd[plane, pl.ds(8, height), :] = jnp.dot(cells, stencil, preferred_element_type=F32)
        columns = columns + edge_columns(cells, plane)
    face[...] = columns.astype(BF16)

    def edge_rows(row):
        own = vol[:, row, :].astype(F32)
        pad = jnp.zeros((rows_out.shape[1] - planes - 2, across), F32)
        ends = [zhalo[slot, row : row + 1, :].astype(F32) for slot in (0, 1)]
        return jnp.concatenate([ends[0], own, ends[1], pad], axis=0).astype(BF16)

    rows_out[0] = edge_rows(0)
    rows_out[1] = edge_rows(height - 1)

    halo = []
    for s, slot in ((1, 0), (-1, 1)):
        sending = (ix + s >= 0) & (ix + s < nx)
        taking = (ix - s >= 0) & (ix - s < nx)
        halo.append((sending, taking, remote(face, faces.at[slot], fs.at[slot], fr.at[slot], (ix + s, iy, iz))))
    for s, side in ((1, 0), (-1, 1)):
        for t in (-1, 0, 1):
            slot = 1 - t
            sending = (iy + s >= 0) & (iy + s < ny) & (ix + t >= 0) & (ix + t < nx)
            taking = (iy - s >= 0) & (iy - s < ny) & (ix - t >= 0) & (ix - t < nx)
            halo.append(
                (sending, taking, remote(rows_out.at[1 - side], rows_in.at[side, slot], rs.at[side, slot], rr.at[side, slot], (ix + t, iy + s, iz)))
            )
    for sending, _, copy in halo:

        @pl.when(sending)
        def _(copy=copy):
            copy.start()

    for b in range(BEFORE + MIDDLE, AHEAD):
        look_block(b)

    for sending, taking, copy in halo:

        @pl.when(taking)
        def _(copy=copy):
            copy.wait_recv()

        @pl.when(sending)
        def _(copy=copy):
            copy.wait_send()

    lane = lax.broadcasted_iota(jnp.int32, (height, across), 1)
    both = jnp.where(lane % 2 == 1, faces[0].astype(F32), faces[1].astype(F32))
    ends = jnp.where((lane == 0) | (lane == across - 1), 1.0, 0.0)
    sign = jnp.where(lane == 0, -1.0, jnp.where(lane == across - 1, 1.0, 0.0))

    def add_columns(z, carry):
        placed = pltpu.roll(both, across - 2 * z - 1, 1)
        xsd[z, pl.ds(8, height), :] += jnp.concatenate([placed * ends, placed * sign], axis=1)
        return carry

    lax.fori_loop(0, planes + 2, add_columns, 0)
    count_rows = rows_out.shape[1]
    for side in (0, 1):
        strip = jnp.dot(rows_in[side, 1], stencil, preferred_element_type=F32)
        left = pltpu.roll(rows_in[side, 0].astype(F32), 1, 1)
        right = pltpu.roll(rows_in[side, 2].astype(F32), across - 1, 1)
        short = lax.broadcasted_iota(jnp.int32, (count_rows, across), 1)
        left = jnp.where(short == 0, left, 0.0)
        right = jnp.where(short == across - 1, right, 0.0)
        strip = strip + jnp.concatenate([left + right, right - left], axis=1)
        row = 7 if side == 0 else 8 + height
        for z in range(planes + 2):
            xsd[z, row : row + 1, :] = strip[z : z + 1]

    shade_scale = (1.0 - ambient) / (32.0 * 3.0**0.5)

    sub = lax.broadcasted_iota(jnp.int32, (8, 2 * across), 0)

    def march(b, own):
        row = pl.multiple_of(start_of(b) + own, 8)

        def gradients(z):
            above = xsd[z, pl.ds(row, 8), :]
            mid = xsd[z, pl.ds(row + 8, 8), :]
            below = xsd[z, pl.ds(row + 16, 8), :]
            up = pltpu.roll(jnp.where(sub == 7, above, mid), 1, 0)
            down = pltpu.roll(jnp.where(sub == 0, below, mid), 7, 0)
            smoothed = up + 2.0 * mid + down
            return smoothed[:, across:], down[:, :across] - up[:, :across], smoothed[:, :across]

        through = jnp.ones((8, across), F32)
        sums = [jnp.zeros((8, across), F32) for _ in range(3)]
        before, here = gradients(0), gradients(1)
        for z in range(planes):
            after = gradients(z + 2)
            grad_x = before[0] + 2.0 * here[0] + after[0]
            grad_y = before[1] + 2.0 * here[1] + after[1]
            grad_z = after[2] - before[2]
            before, here = here, after
            square = (grad_x * grad_x + grad_y * grad_y + grad_z * grad_z) * (1.0 / 1024.0) + grad_floor
            shade = ambient + shade_scale * jnp.abs(grad_x + grad_y + grad_z) * lax.rsqrt(square)
            clear = jnp.exp(look[b, 3, z, pl.ds(own, 8), :] * (-depth_scale / depth))
            weight = through * (1.0 - clear) * shade
            for c in range(3):
                sums[c] = sums[c] + weight * look[b, c, z, pl.ds(own, 8), :]
            through = through * clear
        for c in range(3):
            part[b, c, pl.ds(own, 8), :] = sums[c]
        part[b, 3, pl.ds(own, 8), :] = through

    groups = block // 8
    share = planes // groups

    def render(b):
        def step(n, carry):
            march(b, pl.multiple_of(8 * n, 8))
            if b + AHEAD < 2 * PHASES:
                for k in range(share):
                    look_plane(b + AHEAD, share * n + k)
            return carry

        lax.fori_loop(0, groups, step, 0)

    def to_near(p):
        return remote(part.at[2 * p], recv.at[p, 0], ps.at[p, 0], pr.at[p, 0], (ix, iy, near))

    def to_far(p):
        return remote(pair.at[p], recv.at[p, 1], ps.at[p, 1], pr.at[p, 1], (ix, iy, far))

    def along(p, t):
        tile = code.at[p, bit0, ix]
        return remote(tile, tile, gs.at[p, t - 1], gr.at[p, t - 1], ((ix + t) % nx, iy, iz))

    def hand(p):
        half = code.at[p, bit0]
        return remote(half, half, ns.at[p], nr.at[p], (ix, iy, near))

    def couple(p):
        to_near(p).wait_recv()
        mixed = fold([part[2 * p + 1, c] for c in range(4)], [recv[p, 0, c] for c in range(4)], bit0 == 0)
        for c in range(4):
            pair[p, c] = mixed[c]
        to_far(p).start()

    def composite(p):
        to_far(p).wait_recv()
        quad = fold([pair[p, c] for c in range(4)], [recv[p, 1, c] for c in range(4)], bit1 == 0)
        quad[3] = 1.0 - quad[3]
        encode(quad, code.at[p, bit0, ix])
        for t in range(nx - 1, 0, -1):
            along(p, t).start()

    def show(p, side):
        rows = pl.ds(pl.multiple_of(p * 2 * block + side * block, 16), block)
        for j in range(nx):
            for c in range(4):
                out[c, rows, j * across : (j + 1) * across] = decode(code.at[p, side, j], c)

    def pass_on(p):
        for t in range(1, nx):
            along(p, t).wait_recv()
        hand(p).start()

    def take(p):
        half = code.at[p, 1 - bit0]
        remote(half, half, ns.at[p], nr.at[p], (ix, iy, near)).wait_recv()
        show(p, 1 - bit0)

    def leave(p):
        pass_on(p)
        show(p, bit0)

    last = PHASES - 1
    for b in range(2 * PHASES):
        render(b)
        p = b // 2
        if b % 2 == 0:
            to_near(p).start()
            if p >= 1:
                couple(p - 1)
    couple(last)
    for p in range(PHASES):
        composite(p)
    leave(0)
    for p in range(1, PHASES):
        take(p - 1)
        leave(p)
    take(last)

    for p in range(PHASES):
        for copy in (to_near(p), to_far(p), hand(p)):
            copy.wait_send()
        for t in range(1, nx):
            along(p, t).wait_send()


def shards(volume, hat_center, tf_table):
    planes, height, across = volume.shape
    sizes = tuple(lax.axis_size(a) for a in ("gx", "gy", "gz"))
    nx = sizes[0]
    assert sizes[2] == 4 and across == LANES and height % (32 * PHASES) == 0
    extended_rows = -(-(planes + 2) // 16) * 16
    block = height // (2 * PHASES)
    dma = pltpu.SemaphoreType.DMA
    vmem = pl.BlockSpec(memory_space=pltpu.VMEM)
    hbm = pl.BlockSpec(memory_space=pltpu.MemorySpace.HBM)
    return pl.pallas_call(
        functools.partial(body, sizes),
        out_shape=jax.ShapeDtypeStruct((4, height, across * nx), F32),
        in_specs=[hbm] * 3,
        out_specs=vmem,
        scratch_shapes=[
            pltpu.VMEM((planes, height, across), BF16),
            pltpu.VMEM((1, NBIN), I32),
            pltpu.VMEM((4, NBIN), BF16),
            pltpu.VMEM((32, GROUPS * LANES), F32),
            pltpu.VMEM((planes + 2, height + 16, 2 * across), F32),
            pltpu.VMEM((2 * PHASES, 4, planes, block, across), F32),
            pltpu.VMEM((2, height, across), BF16),
            pltpu.VMEM((height, across), BF16),
            pltpu.VMEM((2, height, across), BF16),
            pltpu.VMEM((2, extended_rows, across), BF16),
            pltpu.VMEM((2, 3, extended_rows, across), BF16),
            pltpu.VMEM((2 * PHASES, 4, block, across), F32),
            pltpu.VMEM((PHASES, 4, block, across), F32),
            pltpu.VMEM((PHASES, 2, 4, block, across), F32),
            pltpu.VMEM((PHASES, 2, nx, 5, block, across), I16),
            dma((3,)),
            dma((2,)), dma((2,)),
            dma((2,)), dma((2,)),
            dma((2, 3)), dma((2, 3)),
            dma((PHASES, 2)), dma((PHASES, 2)),
            dma((PHASES, nx)), dma((PHASES, nx)),
            dma((PHASES,)), dma((PHASES,)),
        ],
        compiler_params=pltpu.CompilerParams(collective_id=0, has_side_effects=True, vmem_limit_bytes=48 << 20),
    )(*(pltpu.with_memory_space_constraint(x, pltpu.MemorySpace.HBM) for x in (volume, hat_center.reshape(1, -1), tf_table)))


def solution(mesh):
    in_specs = (P("gz", "gy", "gx"), P(), P())
    out_specs = P(None, "gy", None)
    return jax.shard_map(shards, mesh=mesh, in_specs=in_specs, out_specs=out_specs, check_vma=False)
```

```python
import functools

import jax
import jax.numpy as jnp
from jax import lax
from jax.experimental import pallas as pl
from jax.experimental.pallas import tpu as pltpu
from jax.sharding import PartitionSpec as P

NBIN = 256
HW = 4

ambient = 0.3
grad_floor = 0.01
depth_scale = 1.5

LANES = 128
GROUPS = 7
PHASES = 4
BEFORE, AFTER = 1, 3
AHEAD = BEFORE + AFTER
STEPS = 65534.0
FINE = 64.0
MESH = pl.DeviceIdType.MESH
F32 = jnp.float32
I16 = jnp.int16
I32 = jnp.int32
BF16 = jnp.bfloat16


def build_tables(center_ref, table_ref, tab):
    centers = center_ref[...].astype(F32)
    wide = table_ref[...].astype(F32)
    copies = jnp.concatenate(
        [jnp.broadcast_to(wide[c : c + 1], (8, NBIN)) for c in range(4)], axis=0
    ).astype(BF16)
    centers = jnp.broadcast_to(centers, (LANES, NBIN))
    row = lax.broadcasted_iota(jnp.int32, (LANES, NBIN), 0).astype(F32)
    away = centers - row

    def hats(level):
        return jnp.maximum(0.0, 1.0 - jnp.abs(level - centers) / HW)

    groups = [
        hats((row + LANES) * (1.0 / (2 * LANES)) * (NBIN - 1)),
        jnp.where(away == -3.0, 0.0, jnp.maximum(0.0, 1.0 - jnp.abs(away) / HW)),
        jnp.where((away == 1.0) | (away == 2.0), 1.0, jnp.where((away == 0.0) | (away == -1.0), -1.0, 0.0)),
        jnp.where(away == 3.0, 1.0, jnp.where(away == -2.0, -1.0, 0.0)),
        jnp.where(away == 4.0, 1.0, 0.0),
        jnp.where(away == -3.0, 1.0, 0.0),
        hats(jnp.full((LANES, NBIN), float(NBIN - 1), F32)),
    ]
    for group, weights in enumerate(groups):
        tab[:, group * LANES : (group + 1) * LANES] = lax.dot_general(
            copies, weights.astype(BF16), (((1,), (1,)), ((), ())), preferred_element_type=F32
        )


def lookup(values, tab):
    level = values * float(NBIN - 1)
    bin_index = level.astype(jnp.int32)
    part_bin = level - bin_index.astype(F32)
    quarter = part_bin * 0.25
    coarse = (quarter + 1.5 * 2.0**15) - 1.5 * 2.0**15
    fine = (quarter + 1.5 * 2.0**14) - 1.5 * 2.0**14
    rising = quarter.astype(BF16).astype(F32)
    falling = ((1.0 - part_bin) * 0.25).astype(BF16).astype(F32)
    low_index = bin_index & (LANES - 1)
    high_index = (values * float(2 * LANES)).astype(jnp.int32) & (LANES - 1)
    upper, top = values >= 0.5, values >= 1.0

    def entry(c, group):
        return tab[8 * c : 8 * c + 8, group * LANES : (group + 1) * LANES]

    out = []
    for c in range(4):
        flat, per_coarse, per_fine, per_rising, per_falling = (
            jnp.take_along_axis(entry(c, 1 + k), low_index, axis=1) for k in range(5)
        )
        total = (flat + coarse * per_coarse) + (fine * per_fine + rising * per_rising + falling * per_falling)
        out.append(total)
    for c in range(4):
        high = jnp.take_along_axis(entry(c, 0), high_index, axis=1)
        out[c] = jnp.where(top, entry(c, 6), jnp.where(upper, high, out[c]))
    return out


def fold(mine, theirs, i_am_front):
    ahead = jnp.where(i_am_front, mine[3], theirs[3])
    mixed = []
    for c in range(3):
        a = jnp.where(i_am_front, mine[c], theirs[c])
        b = jnp.where(i_am_front, theirs[c], mine[c])
        mixed.append(a + ahead * b)
    mixed.append(mine[3] * theirs[3])
    return mixed


def encode(values, code):
    rows, across = values[0].shape
    row = lax.broadcasted_iota(jnp.int32, (rows, across), 0)
    powers = jnp.zeros((rows, across), I32)
    for c in range(4):
        top = jnp.maximum(jnp.max(values[c], axis=0, keepdims=True), 1e-30)
        power = jnp.floor(jnp.log(top) * (FINE * 1.4426950408889634)) + 2.0
        level = values[c] * (jnp.exp2(power * (-1.0 / FINE)) * STEPS) + 0.5
        code[c] = (jnp.minimum(level, STEPS).astype(I32) - 32767).astype(I16)
        powers = jnp.where(row == c, power.astype(I32), powers)
    code[4] = powers.astype(I16)


def decode(code, c):
    power = code[4].astype(I32).astype(F32)[c : c + 1]
    return (code[c].astype(I32).astype(F32) + 32767.0) * (jnp.exp2(power * (1.0 / FINE)) * (1.0 / STEPS))


def body(sizes, vol_in, center_in, table_in, out, vol, center_ref, table_ref, tab, xsd, look, zhalo, face, faces, rows_out, rows_in, part, pair, recv, code,
         ls, zs, zr, fs, fr, rs, rr, ps, pr, gs, gr, ns, nr):
    nx, ny, nz = sizes
    planes, height, across = vol.shape
    ix, iy, iz = lax.axis_index("gx"), lax.axis_index("gy"), lax.axis_index("gz")
    depth = planes * nz
    bit0, bit1 = iz % 2, iz // 2
    near = iz + 1 - 2 * bit0
    far = iz + 2 - 4 * bit1
    diag = near + 2 - 4 * bit1

    loads = [
        pltpu.make_async_copy(src, dst, ls.at[n])
        for n, (src, dst) in enumerate(((vol_in, vol), (center_in, center_ref), (table_in, table_ref)))
    ]
    for load in loads:
        load.start()

    faces[...] = jnp.zeros_like(faces)
    rows_in[...] = jnp.zeros_like(rows_in)
    barrier = pltpu.get_barrier_semaphore()
    for there in (near, far, diag):
        pl.semaphore_signal(barrier, inc=1, device_id=(ix, iy, there), device_id_type=MESH)
    for t in range(1, nx):
        pl.semaphore_signal(barrier, inc=1, device_id=((ix + t) % nx, iy, iz), device_id_type=MESH)
    count = 2 + nx

    def inside(s, t, u):
        x, y, z = ix + t, iy + s, iz + u
        return (x >= 0) & (x < nx) & (y >= 0) & (y < ny) & (z >= 0) & (z < nz)

    corners = [(0, t, u) for t in (-1, 1) for u in (-1, 1)]
    corners += [(s, t, u) for s in (-1, 1) for t in (-1, 0, 1) for u in (-1, 0, 1)]
    for s, t, u in corners:
        there = inside(s, t, u)
        count = count + there.astype(jnp.int32)

        @pl.when(there)
        def _(s=s, t=t, u=u):
            pl.semaphore_signal(barrier, inc=1, device_id=(ix + t, iy + s, iz + u), device_id_type=MESH)

    def remote(src, dst, ssem, rsem, where):
        return pltpu.make_async_remote_copy(
            src_ref=src, dst_ref=dst, send_sem=ssem, recv_sem=rsem, device_id=where, device_id_type=MESH
        )

    front, back = iz > 0, iz < nz - 1
    to_back = remote(vol.at[planes - 1], zhalo.at[0], zs.at[0], zr.at[0], (ix, iy, iz + 1))
    to_front = remote(vol.at[0], zhalo.at[1], zs.at[1], zr.at[1], (ix, iy, iz - 1))

    loads[1].wait()
    loads[2].wait()
    build_tables(center_ref, table_ref, tab)
    loads[0].wait()

    source = lax.broadcasted_iota(jnp.int32, (across, across), 0)
    target = lax.broadcasted_iota(jnp.int32, (across, across), 1)
    gap = source - target
    blur = jnp.where(gap == 0, 2.0, jnp.where(jnp.abs(gap) == 1, 1.0, 0.0))
    slope = jnp.where(gap == 1, 1.0, jnp.where(gap == -1, -1.0, 0.0))
    stencil = jnp.concatenate([blur, slope], axis=1).astype(BF16)

    def edge_columns(cells, plane):
        right = jnp.where((source == across - 1) & (target == 2 * plane + 1), 1.0, 0.0)
        left = jnp.where((source == 0) & (target == 2 * plane), 1.0, 0.0)
        return jnp.dot(cells, (right + left).astype(BF16), preferred_element_type=F32)

    def own_plane(z, acc):
        cells = vol[z]
        xsd[z + 1, pl.ds(8, height), :] = jnp.dot(cells, stencil, preferred_element_type=F32)
        return acc + edge_columns(cells, z + 1)

    def own_planes(n, acc):
        for k in range(4):
            acc = own_plane(4 * n + k, acc)
        return acc

    columns = lax.fori_loop(0, planes // 4, own_planes, jnp.zeros((height, across), F32))
    face[...] = columns.astype(BF16)
    count_rows = rows_out.shape[1]
    for side, row in enumerate((0, height - 1)):
        own = vol[:, row, :].astype(F32)
        if count_rows > planes:
            own = jnp.concatenate([own, jnp.zeros((count_rows - planes, across), F32)], axis=0)
        rows_out[side] = own.astype(BF16)

    block = height // (2 * PHASES)

    def start_of(b):
        side = bit0 if b % 2 else 1 - bit0
        return pl.multiple_of((b // 2) * 2 * block + side * block, 16)

    def look_plane(b, z):
        cells = vol[z, pl.ds(start_of(b), block), :].astype(F32)
        for k in range(block // 8):
            four = lookup(cells[8 * k : 8 * k + 8], tab)
            for c in range(4):
                look[b, c, z, 8 * k : 8 * k + 8, :] = four[c]

    def look_block(b):
        def step(n, carry):
            for k in range(4):
                look_plane(b, 4 * n + k)
            return carry

        lax.fori_loop(0, planes // 4, step, 0)

    for b in range(BEFORE):
        look_block(b)

    pl.semaphore_wait(barrier, count)

    halo = [(back, front, to_back), (front, back, to_front)]
    for u in (0, -1, 1):
        for s, slot in ((1, 0), (-1, 1)):
            copy = remote(face, faces.at[slot, 1 - u], fs.at[slot, 1 - u], fr.at[slot, 1 - u], (ix + s, iy, iz + u))
            halo.append((inside(0, s, u), inside(0, -s, -u), copy))
        for s, side in ((1, 0), (-1, 1)):
            for t in (-1, 0, 1):
                at = (side, 1 - t, 1 - u)
                copy = remote(rows_out.at[1 - side], rows_in.at[at], rs.at[at], rr.at[at], (ix + t, iy + s, iz + u))
                halo.append((inside(s, t, u), inside(-s, -t, -u), copy))
    for sending, _, copy in halo:

        @pl.when(sending)
        def _(copy=copy):
            copy.start()

    for b in range(BEFORE, AHEAD):
        look_block(b)

    for sending, taking, copy in halo:

        @pl.when(taking)
        def _(copy=copy):
            copy.wait_recv()

        @pl.when(sending)
        def _(copy=copy):
            copy.wait_send()

    @pl.when(jnp.logical_not(front))
    def _():
        zhalo[0] = jnp.zeros_like(zhalo[0])

    @pl.when(jnp.logical_not(back))
    def _():
        zhalo[1] = jnp.zeros_like(zhalo[1])

    for slot, plane in ((0, 0), (1, planes + 1)):
        xsd[plane, pl.ds(8, height), :] = jnp.dot(zhalo[slot], stencil, preferred_element_type=F32)

    lane = lax.broadcasted_iota(jnp.int32, (height, across), 1)

    def both_sides(u):
        return jnp.where(lane % 2 == 1, faces[0, u].astype(F32), faces[1, u].astype(F32))

    both = both_sides(1)
    ends = jnp.where((lane == 0) | (lane == across - 1), 1.0, 0.0)
    sign = jnp.where(lane == 0, -1.0, jnp.where(lane == across - 1, 1.0, 0.0))

    def place(z, sides, plane):
        placed = pltpu.roll(sides, across - 2 * plane - 1, 1)
        xsd[z, pl.ds(8, height), :] += jnp.concatenate([placed * ends, placed * sign], axis=1)

    def add_columns(z, carry):
        place(z, both, z)
        return carry

    lax.fori_loop(1, planes + 1, add_columns, 0)
    place(0, both_sides(0), planes)
    place(planes + 1, both_sides(2), 1)
    short = lax.broadcasted_iota(jnp.int32, (count_rows, across), 1)
    for side in (0, 1):
        row = 7 if side == 0 else 8 + height
        for u in range(3):
            strip = jnp.dot(rows_in[side, 1, u], stencil, preferred_element_type=F32)
            left = jnp.where(short == 0, pltpu.roll(rows_in[side, 0, u].astype(F32), 1, 1), 0.0)
            right = jnp.where(short == across - 1, pltpu.roll(rows_in[side, 2, u].astype(F32), across - 1, 1), 0.0)
            strip = strip + jnp.concatenate([left + right, right - left], axis=1)
            for z in range(planes) if u == 1 else ((planes - 1,) if u == 0 else (0,)):
                to = z + 1 if u == 1 else (0 if u == 0 else planes + 1)
                xsd[to, row : row + 1, :] = strip[z : z + 1]

    shade_scale = (1.0 - ambient) / (32.0 * 3.0**0.5)

    sub = lax.broadcasted_iota(jnp.int32, (8, 2 * across), 0)

    def march(b, own):
        row = pl.multiple_of(start_of(b) + own, 8)

        def gradients(z):
            above = xsd[z, pl.ds(row, 8), :]
            mid = xsd[z, pl.ds(row + 8, 8), :]
            below = xsd[z, pl.ds(row + 16, 8), :]
            up = pltpu.roll(jnp.where(sub == 7, above, mid), 1, 0)
            down = pltpu.roll(jnp.where(sub == 0, below, mid), 7, 0)
            smoothed = up + 2.0 * mid + down
            return smoothed[:, across:], down[:, :across] - up[:, :across], smoothed[:, :across]

        through = jnp.ones((8, across), F32)
        sums = [jnp.zeros((8, across), F32) for _ in range(3)]
        before, here = gradients(0), gradients(1)
        for z in range(planes):
            after = gradients(z + 2)
            grad_x = before[0] + 2.0 * here[0] + after[0]
            grad_y = before[1] + 2.0 * here[1] + after[1]
            grad_z = after[2] - before[2]
            before, here = here, after
            square = (grad_x * grad_x + grad_y * grad_y + grad_z * grad_z) * (1.0 / 1024.0) + grad_floor
            shade = ambient + shade_scale * jnp.abs(grad_x + grad_y + grad_z) * lax.rsqrt(square)
            clear = jnp.exp(look[b, 3, z, pl.ds(own, 8), :] * (-depth_scale / depth))
            weight = through * (1.0 - clear) * shade
            for c in range(3):
                sums[c] = sums[c] + weight * look[b, c, z, pl.ds(own, 8), :]
            through = through * clear
        for c in range(3):
            part[b, c, pl.ds(own, 8), :] = sums[c]
        part[b, 3, pl.ds(own, 8), :] = through

    groups = block // 8
    share = planes // groups

    def render(b):
        def step(n, carry):
            march(b, pl.multiple_of(8 * n, 8))
            if b + AHEAD < 2 * PHASES:
                for k in range(share):
                    look_plane(b + AHEAD, share * n + k)
            return carry

        lax.fori_loop(0, groups, step, 0)

    def to_near(p):
        return remote(part.at[2 * p], recv.at[p, 0], ps.at[p, 0], pr.at[p, 0], (ix, iy, near))

    def to_far(p):
        return remote(pair.at[p], recv.at[p, 1], ps.at[p, 1], pr.at[p, 1], (ix, iy, far))

    def along(p, t):
        tile = code.at[p, bit0, ix]
        return remote(tile, tile, gs.at[p, t - 1], gr.at[p, t - 1], ((ix + t) % nx, iy, iz))

    def hand(p):
        half = code.at[p, bit0]
        return remote(half, half, ns.at[p], nr.at[p], (ix, iy, near))

    def couple(p):
        to_near(p).wait_recv()
        mixed = fold([part[2 * p + 1, c] for c in range(4)], [recv[p, 0, c] for c in range(4)], bit0 == 0)
        for c in range(4):
            pair[p, c] = mixed[c]
        to_far(p).start()

    def composite(p):
        to_far(p).wait_recv()
        quad = fold([pair[p, c] for c in range(4)], [recv[p, 1, c] for c in range(4)], bit1 == 0)
        quad[3] = 1.0 - quad[3]
        encode(quad, code.at[p, bit0, ix])
        for t in range(nx - 1, 0, -1):
            along(p, t).start()

    def show(p, side):
        rows = pl.ds(pl.multiple_of(p * 2 * block + side * block, 16), block)
        for j in range(nx):
            for c in range(4):
                out[c, rows, j * across : (j + 1) * across] = decode(code.at[p, side, j], c)

    def pass_on(p):
        for t in range(1, nx):
            along(p, t).wait_recv()
        hand(p).start()

    def take(p):
        half = code.at[p, 1 - bit0]
        remote(half, half, ns.at[p], nr.at[p], (ix, iy, near)).wait_recv()
        show(p, 1 - bit0)

    def leave(p):
        pass_on(p)
        show(p, bit0)

    last = PHASES - 1
    for b in range(2 * PHASES):
        render(b)
        p = b // 2
        if b % 2 == 0:
            to_near(p).start()
            if p >= 1:
                couple(p - 1)
    couple(last)
    for p in range(PHASES):
        composite(p)
    leave(0)
    for p in range(1, PHASES):
        take(p - 1)
        leave(p)
    take(last)

    for p in range(PHASES):
        for copy in (to_near(p), to_far(p), hand(p)):
            copy.wait_send()
        for t in range(1, nx):
            along(p, t).wait_send()


def shards(volume, hat_center, tf_table):
    planes, height, across = volume.shape
    sizes = tuple(lax.axis_size(a) for a in ("gx", "gy", "gz"))
    nx = sizes[0]
    assert sizes[2] == 4 and across == LANES and height % (32 * PHASES) == 0
    padded = -(-planes // 16) * 16
    block = height // (2 * PHASES)
    dma = pltpu.SemaphoreType.DMA
    vmem = pl.BlockSpec(memory_space=pltpu.VMEM)
    hbm = pl.BlockSpec(memory_space=pltpu.MemorySpace.HBM)
    return pl.pallas_call(
        functools.partial(body, sizes),
        out_shape=jax.ShapeDtypeStruct((4, height, across * nx), F32),
        in_specs=[hbm] * 3,
        out_specs=vmem,
        scratch_shapes=[
            pltpu.VMEM((planes, height, across), BF16),
            pltpu.VMEM((1, NBIN), I32),
            pltpu.VMEM((4, NBIN), BF16),
            pltpu.VMEM((32, GROUPS * LANES), F32),
            pltpu.VMEM((planes + 2, height + 16, 2 * across), F32),
            pltpu.VMEM((2 * PHASES, 4, planes, block, across), F32),
            pltpu.VMEM((2, height, across), BF16),
            pltpu.VMEM((height, across), BF16),
            pltpu.VMEM((2, 3, height, across), BF16),
            pltpu.VMEM((2, padded, across), BF16),
            pltpu.VMEM((2, 3, 3, padded, across), BF16),
            pltpu.VMEM((2 * PHASES, 4, block, across), F32),
            pltpu.VMEM((PHASES, 4, block, across), F32),
            pltpu.VMEM((PHASES, 2, 4, block, across), F32),
            pltpu.VMEM((PHASES, 2, nx, 5, block, across), I16),
            dma((3,)),
            dma((2,)), dma((2,)),
            dma((2, 3)), dma((2, 3)),
            dma((2, 3, 3)), dma((2, 3, 3)),
            dma((PHASES, 2)), dma((PHASES, 2)),
            dma((PHASES, nx)), dma((PHASES, nx)),
            dma((PHASES,)), dma((PHASES,)),
        ],
        compiler_params=pltpu.CompilerParams(collective_id=0, has_side_effects=True, vmem_limit_bytes=48 << 20),
    )(*(pltpu.with_memory_space_constraint(x, pltpu.MemorySpace.HBM) for x in (volume, hat_center.reshape(1, -1), tf_table)))


def solution(mesh):
    in_specs = (P("gz", "gy", "gx"), P(), P())
    out_specs = P(None, "gy", None)
    return jax.shard_map(shards, mesh=mesh, in_specs=in_specs, out_specs=out_specs, check_vma=False)
```
